32 devices in a mesh: seg: 8 (over z, x), mp: 4 (over y, core).
Axes of the slice: x: 2, y: 2, z: 4, core: 2. Of those that a mesh axis runs over, the one named last changes fastest.
Arguments:
- patches: bfloat16 [8192, 768], P('seg'), may hold values from -6 to 6
- curve_owner: int32 [8192], P('seg'), may hold values from 0 to 7, as said below
- arrival_slot: int32 [8192], P('seg'), may hold values from 0 to 2047, as said below
- patch_level: int32 [8192], P('seg'), may hold values from 0 to 3
- neighbours: int32 [8192, 16], P('seg'), may hold values from 0 to 8191, as said below
- level_embed: bfloat16 [4, 768], replicated, may hold values from -3 to 3
- norm_gain: float32 [768], replicated, may hold values from 0.5 to 2
- qkv_weight: bfloat16 [768, 3, 768], P(None, None, 'mp')
- out_weight: bfloat16 [768, 768], P('mp'), may hold values from -0.21875 to 0.21875
- cotangent: bfloat16 [8192, 768], P('seg'), may hold values from -6 to 6
Outputs:
- token_grads: float32 [8192, 768], P('seg', 'mp')
- qkv_grad: float32 [768, 3, 768], P(None, None, 'mp')
- out_grad: float32 [768, 768], P('mp')
- gain_grad: float32 [768], P('mp')
The draws below stay inside these ranges and needn't reach their ends.
Inputs may be any that keep to these rules, and one draw needn't show every extreme that they name: `curve_owner`: every device owns exactly 1024 patches. No device holds more than 256 patches with one owner, and in every draw some device holds exactly 256 patches with some owner. `arrival_slot`: entry d * 1024 + p is s * 256 + k: the patch at position p of owner d is the k-th, counted from 0 in row order, of the rows of device s whose owner is d. The entries of one owner are distinct and name every patch it owns. `neighbours`: row p lists positions within 128 of p on the curve, p itself among them; a position may repeat.
All inputs are finite; a program needn't handle non-finite values.
Results may differ from the reference program's by a relative error of at most 0.029.
Values may be sent and summed in bfloat16 or wider, within the bound.
A program may use at most 64 MiB of HBM per device.

```python
import math
import jax
import jax.numpy as jnp
from jax import lax

D = 768
HEADS = 12
DH = 64
LEVELS = 4
TOK_DEV = 1024
R = 128
W = 16
CAP = 256
TOKENS = 8192


def shuffled(subkey):
    return jax.random.permutation(subkey, TOK_DEV)


def routing_tables(key):
    base_key = jax.random.fold_in(key, 11)
    key_order, key_moves, key_rows, key_places = jax.random.split(base_key, 4)
    segments = TOKENS // TOK_DEV
    average = TOK_DEV // segments
    half_count = segments // 2
    others = jax.random.permutation(key_order, segments - 1).astype(jnp.int32)
    others = others + (others >= half_count).astype(jnp.int32)
    shuffle_order = jnp.concatenate([jnp.full((1,), half_count, jnp.int32), others])
    transfers = jax.random.randint(key_moves, (half_count,), 0, average + 1).astype(jnp.int32).at[0].set(average)
    base_counts = jnp.full((segments,), average, jnp.int32)
    base_counts = base_counts.at[shuffle_order[:half_count]].add(transfers).at[shuffle_order[half_count:]].add(-transfers)
    sources = jnp.arange(segments, dtype=jnp.int32)[:, None]
    targets = jnp.arange(segments, dtype=jnp.int32)[None, :]
    counts = base_counts[(targets - sources) % segments]
    bounds = jnp.cumsum(counts, axis=1)
    row_index = jnp.arange(TOK_DEV, dtype=jnp.int32)
    sorted_owner = jnp.sum((bounds[:, None, :] <= row_index[None, :, None]).astype(jnp.int32), axis=2)
    shuffles = jax.vmap(shuffled)(jax.random.split(key_rows, segments))
    owners = jnp.take_along_axis(sorted_owner, shuffles, axis=1)
    onehot = (owners[:, :, None] == jnp.arange(segments, dtype=jnp.int32)[None, None, :]).astype(jnp.int32)
    row_ranks = jnp.sum(onehot * (jnp.cumsum(onehot, axis=1) - onehot), axis=2)
    offsets = jnp.cumsum(counts, axis=0) - counts
    before = jnp.take_along_axis(offsets, owners, axis=1) + row_ranks
    placing = jax.vmap(shuffled)(jax.random.split(key_places, segments))
    positions = placing[owners, before]
    slot_index = (sources * CAP + row_ranks).astype(jnp.int32)
    arrival = jnp.zeros((TOKENS,), jnp.int32).at[(owners * TOK_DEV + positions).reshape(-1)].set(slot_index.reshape(-1))
    return (owners.reshape(-1).astype(jnp.int32), arrival)


def draw_curve_owner(key, part):
    return routing_tables(key)[0]


def draw_arrival_slot(key, part):
    return routing_tables(key)[1]


def draw_neighbours(key, part):
    picks_key = jax.random.fold_in(key, 23)
    bin_width = 2 * R // W
    position = jnp.arange(TOKENS, dtype=jnp.int32)[:, None]
    bin_index = jnp.arange(W, dtype=jnp.int32)[None, :]
    picked = jax.random.randint(picks_key, (TOKENS, W), 0, bin_width).astype(jnp.int32)
    offset = -R + bin_index * bin_width + picked
    offset = jnp.where(bin_index == W // 2, 0, offset)
    target = position + offset
    target = jnp.where((target < 0) | (target >= TOKENS), position - offset, target)
    return target.astype(jnp.int32)


def draw_qkv_weight(key, part):
    key_base = jax.random.fold_in(jax.random.fold_in(key, 31), 0)
    base = jax.random.normal(key_base, (D, 3, HEADS * DH), jnp.float32) * D ** (-0.5)
    return base.astype(jnp.bfloat16)


def set_ends(entries, key, low, top_value):
    longest = entries.shape.index(max(entries.shape))
    spots = []
    for shift in (0, 1):
        where = [jax.random.randint(jax.random.fold_in(key, axis), (), 0, length) for axis, length in enumerate(entries.shape)]
        where[longest] = (where[longest] + shift) % entries.shape[longest]
        spots.append(tuple(where))
    return entries.at[spots[0]].set(low).at[spots[1]].set(top_value)


def block_levels(stream_key, dims, shards, low, top_value):
    level = 1.0
    for dim, blocks in shards:
        heights = jax.random.uniform(jax.random.fold_in(jax.random.fold_in(stream_key, 6), dim), (blocks,), jnp.float32, low / len(shards), top_value / len(shards))
        level = level * jnp.repeat(jnp.exp(heights), dims[dim] // blocks).reshape((-1,) + (1,) * (len(dims) - 1 - dim))
    return level


def scatter_about(stream_key, extent, spread, most, pieces=(), kind=jnp.bfloat16):
    level = block_levels(stream_key, extent, pieces, -0.22, 0.18) if pieces else 1.0
    drawn = jax.random.normal(stream_key, extent, jnp.float32) * spread * level
    return jnp.minimum(jnp.maximum(drawn, -most), most).astype(kind)


def setup_inputs(seed: int = 0) -> dict:
    arg_keys = jax.random.split(jax.random.key(seed), 11)
    patches = scatter_about(arg_keys[0], (TOKENS, D), 1.0, 6.0, ((0, 8),))
    curve_owner = draw_curve_owner(jax.random.fold_in(arg_keys[10], 71), 0)
    arrival_slot = draw_arrival_slot(jax.random.fold_in(arg_keys[10], 71), 0)
    patch_level = set_ends(jax.random.randint(arg_keys[3], (TOKENS,), 0, LEVELS), jax.random.fold_in(arg_keys[3], 1), 0, LEVELS - 1).astype(jnp.int32)
    neighbours = draw_neighbours(jax.random.fold_in(arg_keys[10], 71), 0)
    level_embed = scatter_about(arg_keys[5], (LEVELS, D), 0.5, 3.0)
    norm_gain = jnp.clip(jnp.exp(jax.random.uniform(arg_keys[6], (D,), jnp.float32, math.log(0.5), math.log(2.0))), 0.5, 2.0)
    qkv_weight = draw_qkv_weight(jax.random.fold_in(arg_keys[10], 71), 0)
    out_weight = scatter_about(arg_keys[8], (HEADS * DH, D), (HEADS * DH) ** -0.5, 0.21875, ((0, 4),))
    cotangent = scatter_about(arg_keys[9], (TOKENS, D), 1.0, 6.0, ((0, 8),))
    return dict(patches=patches, curve_owner=curve_owner, arrival_slot=arrival_slot, patch_level=patch_level, neighbours=neighbours, level_embed=level_embed, norm_gain=norm_gain, qkv_weight=qkv_weight, out_weight=out_weight, cotangent=cotangent)


EPSILON = 1e-06

def source_rows(curve_owner, arrival_slot):
    segments = TOKENS // TOK_DEV
    owners = curve_owner.reshape(segments, TOK_DEV)
    onehot = (owners[:, :, None] == jnp.arange(segments, dtype=jnp.int32)[None, None, :]).astype(jnp.int32)
    row_ranks = lax.optimization_barrier(jnp.sum(onehot * (jnp.cumsum(onehot, axis=1) - onehot), axis=2))
    sources = jnp.arange(segments, dtype=jnp.int32)[:, None]
    places = ((owners * segments + sources) * CAP + row_ranks).reshape(-1).astype(jnp.int32)
    lookup = jnp.zeros((segments * segments * CAP,), jnp.int32).at[places].set(jnp.arange(TOKENS, dtype=jnp.int32))
    owner_row = jnp.arange(TOKENS, dtype=jnp.int32) // TOK_DEV
    return lookup[(owner_row * (segments * CAP) + arrival_slot).astype(jnp.int32)]

def reference(patches, curve_owner, arrival_slot, patch_level, neighbours, level_embed, norm_gain, qkv_weight, out_weight, cotangent):
    all_width = HEADS * DH
    routed = patches[source_rows(curve_owner, arrival_slot)]
    embedded = routed.astype(jnp.float32) + level_embed.astype(jnp.float32)[patch_level]
    inv_rms = lax.rsqrt(lax.optimization_barrier(jnp.mean(embedded * embedded, axis=1, keepdims=True)) + EPSILON)
    normed = embedded * inv_rms
    hidden = (normed * norm_gain).astype(jnp.bfloat16)
    project = jnp.dot(hidden, qkv_weight.reshape(D, 3 * all_width), preferred_element_type=jnp.float32)
    project = project.astype(jnp.bfloat16).reshape(TOKENS, 3, HEADS, DH)
    queries = project[:, 0]
    key_pad = jnp.pad(project[:, 1], ((R, R), (0, 0), (0, 0)))
    value_pad = jnp.pad(project[:, 2], ((R, R), (0, 0), (0, 0)))
    grad_out = jnp.dot(cotangent, out_weight.T, preferred_element_type=jnp.float32).astype(jnp.bfloat16).reshape(TOKENS, HEADS, DH)
    block_rows = min(TOK_DEV, 512)
    key_span = block_rows + 2 * R
    score_scale = DH ** (-0.5)

    def one_block(carried, block_start):
        grad_keys, grad_values = carried
        query_block = lax.dynamic_slice_in_dim(queries, block_start, block_rows, 0).astype(jnp.float32)
        key_block = lax.dynamic_slice_in_dim(key_pad, block_start, key_span, 0).astype(jnp.float32)
        value_block = lax.dynamic_slice_in_dim(value_pad, block_start, key_span, 0).astype(jnp.float32)
        positions = block_start - R + jnp.arange(key_span, dtype=jnp.int32)
        listed = lax.dynamic_slice_in_dim(neighbours, block_start, block_rows, 0)
        allowed = jnp.any(listed[:, :, None] == positions[None, None, :], axis=1)[None]
        scores = jnp.einsum('qhd,khd->hqk', query_block, key_block) * score_scale
        row_top = lax.optimization_barrier(jnp.max(jnp.where(allowed, scores, -jnp.inf), axis=2, keepdims=True))
        exponent = jnp.where(allowed, jnp.exp(scores - row_top), 0.0)
        probability = exponent / lax.optimization_barrier(jnp.sum(exponent, axis=2, keepdims=True))
        weights = lax.optimization_barrier(probability.astype(jnp.bfloat16)).astype(jnp.float32)
        out_block = jnp.einsum('hqk,khd->qhd', weights, value_block).astype(jnp.bfloat16)
        out_wide = lax.optimization_barrier(out_block).astype(jnp.float32)
        grad_block = lax.dynamic_slice_in_dim(grad_out, block_start, block_rows, 0).astype(jnp.float32)
        row_delta = lax.optimization_barrier(jnp.sum(grad_block * out_wide, axis=2)).T[:, :, None]
        grad_prob = jnp.einsum('qhd,khd->hqk', grad_block, value_block)
        dscore = (probability * (grad_prob - row_delta) * score_scale).astype(jnp.bfloat16)
        dscore = lax.optimization_barrier(dscore).astype(jnp.float32)
        dquery = jnp.einsum('hqk,khd->qhd', dscore, key_block)
        grad_key = jnp.einsum('hqk,qhd->khd', dscore, query_block)
        dvalue = jnp.einsum('hqk,qhd->khd', weights, grad_block)
        old_keys = lax.dynamic_slice_in_dim(grad_keys, block_start, key_span, 0)
        old_values = lax.dynamic_slice_in_dim(grad_values, block_start, key_span, 0)
        grad_keys = lax.dynamic_update_slice_in_dim(grad_keys, old_keys + grad_key, block_start, 0)
        grad_values = lax.dynamic_update_slice_in_dim(grad_values, old_values + dvalue, block_start, 0)
        return ((grad_keys, grad_values), (out_block, dquery))
    block_starts = jnp.arange(TOKENS // block_rows, dtype=jnp.int32) * block_rows
    zeros_init = jnp.zeros((TOKENS + 2 * R, HEADS, DH), jnp.float32)
    (grad_keys, grad_values), (attended, query_grads) = lax.scan(one_block, (zeros_init, zeros_init), block_starts)
    attended = attended.reshape(TOKENS, all_width)
    query_grads = query_grads.reshape(TOKENS, HEADS, DH)
    grad_qkv = jnp.stack([query_grads, grad_keys[R:R + TOKENS], grad_values[R:R + TOKENS]], axis=1)
    grad_qkv = grad_qkv.astype(jnp.bfloat16).reshape(TOKENS, 3 * all_width)
    factor = TOKENS ** (-0.5)
    qkv_grad = (jnp.dot(hidden.T, grad_qkv, preferred_element_type=jnp.float32) * factor).reshape(D, 3, all_width)
    out_grad = jnp.dot(attended.T, cotangent, preferred_element_type=jnp.float32) * factor
    grad_hidden = jnp.dot(grad_qkv, qkv_weight.reshape(D, 3 * all_width).T, preferred_element_type=jnp.float32)
    gain_grad = lax.optimization_barrier(jnp.sum(grad_hidden * normed, axis=0)) * factor
    scaled = grad_hidden * norm_gain
    token_grads = cotangent.astype(jnp.float32) + inv_rms * (scaled - normed * lax.optimization_barrier(jnp.mean(scaled * normed, axis=1, keepdims=True)))
    return (token_grads, qkv_grad, out_grad, gain_grad)
```

```python
import jax
import jax.numpy as jnp
from jax import lax
from jax.experimental import pallas as pl
from jax.experimental.pallas import tpu as pltpu
from jax.sharding import PartitionSpec as P

DH = 64
R = 128
EPSILON = 1e-06
MESH = pl.DeviceIdType.MESH


def exchange(collective_id, *parts):
    arrays = [part[0] for part in parts]
    axes = sorted({part[1] for part in parts})
    counts = {axis: lax.axis_size(axis) for axis in axes}
    shapes = []
    for array, axis, kind in parts:
        lead = (counts[axis],) if kind == "gather" else ()
        shapes.append(jax.ShapeDtypeStruct(lead + array.shape, array.dtype))
    number = len(parts)
    copies = [counts[axis] if kind in ("scatter", "gather") else 1 for _, axis, kind in parts]

    def body(*refs):
        sources, targets = refs[:number], refs[number : 2 * number]
        sends = refs[2 * number : 3 * number]
        receives = refs[3 * number : 4 * number]
        barrier = pltpu.get_barrier_semaphore()
        expected = 0
        for axis in axes:
            here, count = lax.axis_index(axis), counts[axis]
            for step in range(1, count):
                pl.semaphore_signal(
                    barrier,
                    inc=1,
                    device_id={axis: lax.rem(here + step, count)},
                    device_id_type=MESH,
                )
                expected += 1
        pl.semaphore_wait(barrier, expected)
        started = []
        for index, (_, axis, kind) in enumerate(parts):
            source, target = sources[index], targets[index]
            here, count = lax.axis_index(axis), counts[axis]
            if kind in ("next", "prev"):
                step = 1 if kind == "next" else count - 1
                steps = [step]
            else:
                steps = list(range(1, count))
            for slot, step in enumerate(steps):
                peer = lax.rem(here + step, count)
                block = source.at[peer] if kind == "scatter" else source
                place = target if kind in ("next", "prev") else target.at[here]
                copy = pltpu.make_async_remote_copy(
                    src_ref=block,
                    dst_ref=place,
                    send_sem=sends[index].at[slot],
                    recv_sem=receives[index].at[slot],
                    device_id={axis: peer},
                    device_id_type=MESH,
                )
                copy.start()
                started.append(copy)
        for index, (_, axis, kind) in enumerate(parts):
            if kind in ("scatter", "gather"):
                here, count = lax.axis_index(axis), counts[axis]
                source = sources[index]
                block = source.at[here] if kind == "scatter" else source
                own = pltpu.make_async_copy(
                    block, targets[index].at[here], sends[index].at[count - 1]
                )
                own.start()
                started.append(own)
        for copy in started:
            copy.wait()

    return pl.pallas_call(
        body,
        out_shape=shapes,
        in_specs=[pl.BlockSpec(memory_space=pltpu.VMEM)] * number,
        out_specs=[pl.BlockSpec(memory_space=pltpu.VMEM)] * number,
        scratch_shapes=[pltpu.SemaphoreType.DMA((n,)) for n in copies] * 2,
        compiler_params=pltpu.CompilerParams(collective_id=collective_id, has_side_effects=True),
        name=f"exchange_{collective_id}",
    )(*arrays)


def attention(queries, extended, grad_out, neighbours):
    tok_rows, width = queries.shape
    heads = width // DH
    rows = R
    span = rows + 2 * R
    scale = DH ** (-0.5)

    def body(q_ref, kv_ref, g_ref, near_ref, out_ref, dq_ref, grad_ref):
        step = pl.program_id(0)

        @pl.when(step == 0)
        def _():
            grad_ref[...] = jnp.zeros_like(grad_ref)

        start = pl.multiple_of(step * rows, rows)
        first = lax.axis_index("seg") * tok_rows - R + step * rows
        near = near_ref[...] - first
        places = lax.broadcasted_iota(jnp.int32, (rows, span), 1)
        allowed = near[:, 0:1] == places
        for column in range(1, near.shape[1]):
            allowed = allowed | (near[:, column : column + 1] == places)
        window = kv_ref[pl.ds(start, span), :]
        outs, dqs, dks, dvs = [], [], [], []
        for head in range(heads):
            part = slice(head * DH, (head + 1) * DH)
            q, g = q_ref[:, part], g_ref[:, part]
            k = window[:, part]
            v = window[:, width + head * DH : width + (head + 1) * DH]
            across = (((1,), (1,)), ((), ()))
            down = (((0,), (0,)), ((), ()))
            s = lax.dot_general(q, k, across, preferred_element_type=jnp.float32) * scale
            s = jnp.where(allowed, s, -jnp.inf)
            e = jnp.exp(s - jnp.max(s, axis=1, keepdims=True))
            p = e * (1.0 / jnp.sum(e, axis=1, keepdims=True))
            w = p.astype(jnp.bfloat16)
            o = jnp.dot(w, v, preferred_element_type=jnp.float32).astype(jnp.bfloat16)
            delta = jnp.sum(
                g.astype(jnp.float32) * o.astype(jnp.float32), axis=1, keepdims=True
            )
            gp = lax.dot_general(g, v, across, preferred_element_type=jnp.float32)
            ds = (p * (gp - delta) * scale).astype(jnp.bfloat16)
            outs.append(o)
            dqs.append(jnp.dot(ds, k, preferred_element_type=jnp.float32).astype(jnp.bfloat16))
            dks.append(lax.dot_general(ds, q, down, preferred_element_type=jnp.float32))
            dvs.append(lax.dot_general(w, g, down, preferred_element_type=jnp.float32))
        out_ref[...] = jnp.concatenate(outs, axis=1)
        dq_ref[...] = jnp.concatenate(dqs, axis=1)
        grad_ref[pl.ds(start, span), :] += jnp.concatenate(dks + dvs, axis=1)

    by_row = pl.BlockSpec((rows, width), lambda i: (i, 0))
    whole = pl.BlockSpec(extended.shape, lambda i: (0, 0))
    return pl.pallas_call(
        body,
        grid=(tok_rows // rows,),
        in_specs=[
            by_row,
            whole,
            by_row,
            pl.BlockSpec((rows, neighbours.shape[1]), lambda i: (i, 0)),
        ],
        out_specs=[by_row, by_row, whole],
        out_shape=[
            jax.ShapeDtypeStruct((tok_rows, width), jnp.bfloat16),
            jax.ShapeDtypeStruct((tok_rows, width), jnp.bfloat16),
            jax.ShapeDtypeStruct(extended.shape, jnp.float32),
        ],
        name="window_attention",
    )(queries, extended, grad_out, neighbours)


def per_device(
    patches,
    curve_owner,
    arrival_slot,
    patch_level,
    neighbours,
    level_embed,
    norm_gain,
    qkv_weight,
    out_weight,
    cotangent,
):
    segments = lax.axis_size("seg")
    shares = lax.axis_size("mp")
    tok_rows, model_width = patches.shape
    local_width = qkv_weight.shape[2]
    capacity = 2 * tok_rows // segments
    share_width = model_width // shares
    first_column = lax.axis_index("mp") * share_width
    bf16, f32 = jnp.bfloat16, jnp.float32

    def columns_here(array, dim):
        return lax.dynamic_slice_in_dim(array, first_column, share_width, dim)

    row = jnp.arange(tok_rows, dtype=jnp.int32)
    owner_hot = curve_owner[:, None] == jnp.arange(segments, dtype=jnp.int32)[None, :]
    before = (row[None, :] < row[:, None]).astype(bf16)
    counted = jnp.dot(before, owner_hot.astype(bf16), preferred_element_type=f32)
    row_ranks = jnp.sum(jnp.where(owner_hot, counted, 0.0), axis=1).astype(jnp.int32)
    slot_index = curve_owner * capacity + row_ranks
    slots = jnp.arange(segments * capacity, dtype=jnp.int32)
    sent_hot = (slot_index[:, None] == slots[None, :]).astype(bf16)
    packed = lax.dot_general(
        columns_here(patches, 1), sent_hot, (((0,), (0,)), ((), ())), preferred_element_type=f32
    ).astype(bf16)
    packed = packed.reshape(share_width, segments, capacity).transpose(1, 0, 2)
    (arrived,) = exchange(0, (packed, "seg", "scatter"))
    arrived = arrived.transpose(1, 0, 2).reshape(share_width, segments * capacity)
    taken_hot = (slots[:, None] == arrival_slot[None, :]).astype(bf16)
    routed = jnp.dot(arrived, taken_hot, preferred_element_type=f32).astype(bf16)
    (routed,) = exchange(1, (routed, "mp", "gather"))
    routed = routed.reshape(model_width, tok_rows)

    levels = jnp.arange(level_embed.shape[0], dtype=jnp.int32)
    level_hot = (levels[:, None] == patch_level[None, :]).astype(bf16)
    embedded = routed.astype(f32) + lax.dot_general(
        level_embed, level_hot, (((0,), (0,)), ((), ())), preferred_element_type=f32
    )
    inv_rms = lax.rsqrt(jnp.mean(embedded * embedded, axis=0, keepdims=True) + EPSILON)
    normed = embedded * inv_rms
    gain = norm_gain[:, None]
    hidden = (normed * gain).astype(bf16)
    flat_weight = qkv_weight.reshape(model_width, 3 * local_width)
    project = lax.dot_general(
        hidden, flat_weight, (((0,), (0,)), ((), ())), preferred_element_type=f32
    ).astype(bf16)
    queries = project[:, :local_width]
    key_value = project[:, local_width:]
    from_left, from_right = exchange(
        2, (key_value[tok_rows - R :], "seg", "next"), (key_value[:R], "seg", "prev")
    )
    extended = jnp.concatenate([from_left, key_value, from_right], axis=0)
    grad_out = lax.dot_general(
        cotangent, out_weight, (((1,), (1,)), ((), ())), preferred_element_type=f32
    ).astype(bf16)
    attended, grad_query, grad_ext = attention(queries, extended, grad_out, neighbours)
    rim_left, rim_right = exchange(
        3,
        (grad_ext[tok_rows + R :].astype(bf16), "seg", "next"),
        (grad_ext[:R].astype(bf16), "seg", "prev"),
    )
    grad_kv = jnp.concatenate(
        [
            grad_ext[R : 2 * R] + rim_left.astype(f32),
            grad_ext[2 * R : tok_rows],
            grad_ext[tok_rows : tok_rows + R] + rim_right.astype(f32),
        ],
        axis=0,
    )
    grad_qkv = jnp.concatenate([grad_query, grad_kv.astype(bf16)], axis=1)

    qkv_part = lax.dot_general(
        grad_qkv, hidden, (((0,), (1,)), ((), ())), preferred_element_type=f32
    ).astype(bf16)
    out_part = lax.dot_general(
        attended, cotangent, (((0,), (0,)), ((), ())), preferred_element_type=f32
    ).astype(bf16)
    weight_rows = 4 * local_width
    weight_part = jnp.concatenate([qkv_part, out_part], axis=0).reshape(
        segments, weight_rows // segments, model_width
    )
    hidden_part = lax.dot_general(
        flat_weight, grad_qkv, (((1,), (1,)), ((), ())), preferred_element_type=f32
    )
    product = hidden_part * normed
    dots_part = jnp.sum(product * gain, axis=0, keepdims=True)
    gain_part = jnp.sum(product, axis=1).reshape(shares, 1, share_width)
    shared_hidden = hidden_part.astype(bf16).reshape(shares, share_width, tok_rows)
    weights_in, hidden_in, dots_in, gain_in = exchange(
        4,
        (weight_part, "seg", "scatter"),
        (shared_hidden, "mp", "scatter"),
        (dots_part, "mp", "gather"),
        (gain_part, "mp", "scatter"),
    )
    factor = (tok_rows * segments) ** (-0.5)
    weight_sum = (jnp.sum(weights_in.astype(f32), axis=0) * factor).astype(bf16)
    gain_sum = jnp.sum(gain_in, axis=0) * factor
    weights_all, gains_all = exchange(5, (weight_sum, "seg", "gather"), (gain_sum, "seg", "gather"))
    weights_all = weights_all.reshape(weight_rows, model_width).astype(f32)
    qkv_grad = weights_all[: 3 * local_width].T.reshape(model_width, 3, local_width)
    out_grad = weights_all[3 * local_width :]
    gain_grad = jnp.sum(gains_all, axis=0).reshape(share_width)

    grad_hidden = jnp.sum(hidden_in.astype(f32), axis=0)
    mean = jnp.sum(dots_in, axis=0) / model_width
    scaled = grad_hidden * columns_here(gain, 0)
    token_grads = columns_here(cotangent, 1).astype(f32) + (
        inv_rms * (scaled - columns_here(normed, 0) * mean)
    ).T
    return (token_grads, qkv_grad, out_grad, gain_grad)


def solution(mesh):
    placed = (
        P("seg", None),
        P("seg"),
        P("seg"),
        P("seg"),
        P("seg", None),
        P(),
        P(),
        P(None, None, "mp"),
        P("mp", None),
        P("seg", None),
    )
    return jax.shard_map(
        per_device,
        mesh=mesh,
        in_specs=placed,
        out_specs=(P("seg", "mp"), P(None, None, "mp"), P("mp", None), P("mp")),
        check_vma=False,
    )
```

```python
import jax
import jax.numpy as jnp
from jax import lax
from jax.experimental import pallas as pl
from jax.experimental.pallas import tpu as pltpu
from jax.sharding import PartitionSpec as P

DH = 64
R = 128
EPSILON = 1e-06
MESH = pl.DeviceIdType.MESH


def exchange(collective_id, *parts):
    arrays = [part[0] for part in parts]
    axes = sorted({part[1] for part in parts})
    counts = {axis: lax.axis_size(axis) for axis in axes}
    shapes, slots = [], []
    for array, axis, kind in parts:
        count = counts[axis]
        lead = (count,) if kind in ("gather", "direct") else ()
        shapes.append(jax.ShapeDtypeStruct(lead + array.shape, array.dtype))
        slots.append({"scatter": count, "direct": count, "gather": 2 * count}.get(kind, 1))
    number = len(parts)

    def remote(source, target, sends, receives, slot, axis, peer):
        return pltpu.make_async_remote_copy(
            src_ref=source,
            dst_ref=target,
            send_sem=sends.at[slot],
            recv_sem=receives.at[slot],
            device_id={axis: peer},
            device_id_type=MESH,
        )

    def scatter(source, target, sends, receives, axis, split):
        here, count = lax.axis_index(axis), counts[axis]
        copies = []
        for step in range(1, count):
            peer = lax.rem(here + step, count)
            block = source.at[peer] if split else source
            copies.append(remote(block, target.at[here], sends, receives, step, axis, peer))
        block = source.at[here] if split else source
        copies.append(pltpu.make_async_copy(block, target.at[here], sends.at[0]))
        for copy in copies:
            copy.start()

        def finish():
            for copy in copies:
                copy.wait()

        return (lambda: None), finish

    def shift(source, target, sends, receives, axis, forward):
        here, count = lax.axis_index(axis), counts[axis]
        step = 1 if forward else -1
        peer = lax.rem(here + step + count, count)
        has_peer = here < count - 1 if forward else here > 0
        has_source = here > 0 if forward else here < count - 1
        copy = remote(source, target, sends, receives, 0, axis, peer)
        pl.when(has_peer)(copy.start)

        def finish():
            pl.when(has_peer)(copy.wait_send)
            pl.when(has_source)(copy.wait_recv)

        return (lambda: None), finish

    def gather(source, target, sends, receives, axis):
        here, count = lax.axis_index(axis), counts[axis]
        line = count // 2
        outer = here // 2
        partner = here + 1 - 2 * lax.rem(here, 2)
        ahead = lax.rem(here + 2, count)
        behind = lax.rem(here + count - 2, count)
        own = pltpu.make_async_copy(source, target.at[here], sends.at[0])

        def block(shift):
            return target.at[lax.rem(here + 2 * shift + count, count)]

        def hand_on(shift, direction, step):
            peer = ahead if direction > 0 else behind
            slot = step if direction > 0 else line + step
            taken = source if shift == 0 else block(shift)
            return remote(taken, block(shift), sends, receives, slot, axis, peer)

        def hand_over(shift):
            slot = 2 * line + (shift if shift >= 0 else line - 1 - shift)
            taken = source if shift == 0 else block(shift)
            return remote(taken, block(shift), sends, receives, slot, axis, partner)

        def there(shift):
            place = outer + shift
            return (place >= 0) if shift < 0 else (place < line)

        if line > 1:
            pl.when(there(1))(hand_on(0, 1, 1).start)
            pl.when(there(-1))(hand_on(0, -1, 1).start)
        hand_over(0).start()
        own.start()

        def relay():
            for step in range(1, line):
                for direction in (1, -1):
                    came = -direction * step

                    @pl.when(there(came))
                    def _():
                        hand_on(came, direction, step).wait_recv()
                        if step < line - 1:
                            pl.when(there(direction))(hand_on(came, direction, step + 1).start)
                        hand_over(came).start()

        def finish():
            for step in range(1, line):
                for direction in (1, -1):
                    came = -direction * (step - 1)

                    @pl.when(there(direction) if step == 1 else there(came) & there(direction))
                    def _():
                        hand_on(came, direction, step).wait_send()

                    pl.when(there(direction * step))(hand_over(direction * step).wait)
            hand_over(0).wait()
            own.wait()

        return relay, finish

    def body(*refs):
        groups = [refs[i * number : (i + 1) * number] for i in range(4)]
        barrier = pltpu.get_barrier_semaphore()
        expected = 0
        for axis in axes:
            here, count = lax.axis_index(axis), counts[axis]
            for step in range(1, count):
                pl.semaphore_signal(
                    barrier,
                    inc=1,
                    device_id={axis: lax.rem(here + step, count)},
                    device_id_type=MESH,
                )
                expected += 1
        pl.semaphore_wait(barrier, expected)
        pending = []
        for (_, axis, kind), *held in zip(parts, *groups):
            if kind in ("scatter", "direct"):
                pending.append(scatter(*held, axis, kind == "scatter"))
            elif kind == "gather":
                pending.append(gather(*held, axis))
            else:
                pending.append(shift(*held, axis, kind == "next"))
        for relay, _ in pending:
            relay()
        for _, finish in pending:
            finish()

    return pl.pallas_call(
        body,
        out_shape=shapes,
        in_specs=[pl.BlockSpec(memory_space=pltpu.VMEM)] * number,
        out_specs=[pl.BlockSpec(memory_space=pltpu.VMEM)] * number,
        scratch_shapes=[pltpu.SemaphoreType.DMA((n,)) for n in slots] * 2,
        compiler_params=pltpu.CompilerParams(collective_id=collective_id, has_side_effects=True),
        name=f"exchange_{collective_id}",
    )(*arrays)


def attention(queries, extended, grad_out, neighbours):
    tok_rows, width = queries.shape
    heads = width // DH
    rows = R
    span = rows + 2 * R
    scale = DH ** (-0.5)

    def body(q_ref, kv_ref, g_ref, near_ref, out_ref, dq_ref, grad_ref):
        step = pl.program_id(0)

        @pl.when(step == 0)
        def _():
            grad_ref[...] = jnp.zeros_like(grad_ref)

        start = pl.multiple_of(step * rows, rows)
        first = lax.axis_index("seg") * tok_rows - R + step * rows
        near = near_ref[...] - first
        places = lax.broadcasted_iota(jnp.int32, (rows, span), 1)
        allowed = near[:, 0:1] == places
        for column in range(1, near.shape[1]):
            allowed = allowed | (near[:, column : column + 1] == places)
        window = kv_ref[pl.ds(start, span), :]
        outs, dqs, dks, dvs = [], [], [], []
        for head in range(heads):
            part = slice(head * DH, (head + 1) * DH)
            q, g = q_ref[:, part], g_ref[:, part]
            k = window[:, part]
            v = window[:, width + head * DH : width + (head + 1) * DH]
            across = (((1,), (1,)), ((), ()))
            down = (((0,), (0,)), ((), ()))
            s = lax.dot_general(q, k, across, preferred_element_type=jnp.float32) * scale
            s = jnp.where(allowed, s, -jnp.inf)
            e = jnp.exp(s - jnp.max(s, axis=1, keepdims=True))
            p = e * (1.0 / jnp.sum(e, axis=1, keepdims=True))
            w = p.astype(jnp.bfloat16)
            o = jnp.dot(w, v, preferred_element_type=jnp.float32).astype(jnp.bfloat16)
            delta = jnp.sum(
                g.astype(jnp.float32) * o.astype(jnp.float32), axis=1, keepdims=True
            )
            gp = lax.dot_general(g, v, across, preferred_element_type=jnp.float32)
            ds = (p * (gp - delta) * scale).astype(jnp.bfloat16)
            outs.append(o)
            dqs.append(jnp.dot(ds, k, preferred_element_type=jnp.float32).astype(jnp.bfloat16))
            dks.append(lax.dot_general(ds, q, down, preferred_element_type=jnp.float32))
            dvs.append(lax.dot_general(w, g, down, preferred_element_type=jnp.float32))
        out_ref[...] = jnp.concatenate(outs, axis=1)
        dq_ref[...] = jnp.concatenate(dqs, axis=1)
        grad_ref[pl.ds(start, span), :] += jnp.concatenate(dks + dvs, axis=1)

    by_row = pl.BlockSpec((rows, width), lambda i: (i, 0))
    whole = pl.BlockSpec(extended.shape, lambda i: (0, 0))
    return pl.pallas_call(
        body,
        grid=(tok_rows // rows,),
        in_specs=[
            by_row,
            whole,
            by_row,
            pl.BlockSpec((rows, neighbours.shape[1]), lambda i: (i, 0)),
        ],
        out_specs=[by_row, by_row, whole],
        out_shape=[
            jax.ShapeDtypeStruct((tok_rows, width), jnp.bfloat16),
            jax.ShapeDtypeStruct((tok_rows, width), jnp.bfloat16),
            jax.ShapeDtypeStruct(extended.shape, jnp.float32),
        ],
        name="window_attention",
    )(queries, extended, grad_out, neighbours)


def per_device(
    patches,
    curve_owner,
    arrival_slot,
    patch_level,
    neighbours,
    level_embed,
    norm_gain,
    qkv_weight,
    out_weight,
    cotangent,
):
    segments = lax.axis_size("seg")
    shares = lax.axis_size("mp")
    tok_rows, model_width = patches.shape
    local_width = qkv_weight.shape[2]
    capacity = 2 * tok_rows // segments
    share_width = model_width // shares
    first_column = lax.axis_index("mp") * share_width
    bf16, f32 = jnp.bfloat16, jnp.float32

    def columns_here(array, dim):
        return lax.dynamic_slice_in_dim(array, first_column, share_width, dim)

    row = jnp.arange(tok_rows, dtype=jnp.int32)
    owner_hot = curve_owner[:, None] == jnp.arange(segments, dtype=jnp.int32)[None, :]
    before = (row[None, :] < row[:, None]).astype(bf16)
    counted = jnp.dot(before, owner_hot.astype(bf16), preferred_element_type=f32)
    row_ranks = jnp.sum(jnp.where(owner_hot, counted, 0.0), axis=1).astype(jnp.int32)
    slot_index = curve_owner * capacity + row_ranks
    slots = jnp.arange(segments * capacity, dtype=jnp.int32)
    sent_hot = (slot_index[:, None] == slots[None, :]).astype(bf16)
    packed = lax.dot_general(
        columns_here(patches, 1), sent_hot, (((0,), (0,)), ((), ())), preferred_element_type=f32
    ).astype(bf16)
    packed = packed.reshape(share_width, segments, capacity).transpose(1, 0, 2)
    (arrived,) = exchange(0, (packed, "seg", "scatter"))
    arrived = arrived.transpose(1, 0, 2).reshape(share_width, segments * capacity)
    taken_hot = (slots[:, None] == arrival_slot[None, :]).astype(bf16)
    routed = jnp.dot(arrived, taken_hot, preferred_element_type=f32).astype(bf16)
    (routed,) = exchange(1, (routed, "mp", "gather"))
    routed = routed.reshape(model_width, tok_rows)

    levels = jnp.arange(level_embed.shape[0], dtype=jnp.int32)
    level_hot = (levels[:, None] == patch_level[None, :]).astype(bf16)
    embedded = routed.astype(f32) + lax.dot_general(
        level_embed, level_hot, (((0,), (0,)), ((), ())), preferred_element_type=f32
    )
    inv_rms = lax.rsqrt(jnp.mean(embedded * embedded, axis=0, keepdims=True) + EPSILON)
    normed = embedded * inv_rms
    gain = norm_gain[:, None]
    hidden = (normed * gain).astype(bf16)
    flat_weight = qkv_weight.reshape(model_width, 3 * local_width)
    project = lax.dot_general(
        hidden, flat_weight, (((0,), (0,)), ((), ())), preferred_element_type=f32
    ).astype(bf16)
    queries = project[:, :local_width]
    key_value = project[:, local_width:]
    from_left, from_right = exchange(
        2, (key_value[tok_rows - R :], "seg", "next"), (key_value[:R], "seg", "prev")
    )
    segment = lax.axis_index("seg")
    from_left = jnp.where(segment > 0, from_left, 0)
    from_right = jnp.where(segment < segments - 1, from_right, 0)
    extended = jnp.concatenate([from_left, key_value, from_right], axis=0)
    grad_out = lax.dot_general(
        cotangent, out_weight, (((1,), (1,)), ((), ())), preferred_element_type=f32
    ).astype(bf16)
    attended, grad_query, grad_ext = attention(queries, extended, grad_out, neighbours)
    rim_left, rim_right = exchange(
        3,
        (grad_ext[tok_rows + R :].astype(bf16), "seg", "next"),
        (grad_ext[:R].astype(bf16), "seg", "prev"),
    )
    rim_left = jnp.where(segment > 0, rim_left, 0)
    rim_right = jnp.where(segment < segments - 1, rim_right, 0)
    grad_kv = jnp.concatenate(
        [
            grad_ext[R : 2 * R] + rim_left.astype(f32),
            grad_ext[2 * R : tok_rows],
            grad_ext[tok_rows : tok_rows + R] + rim_right.astype(f32),
        ],
        axis=0,
    )
    grad_qkv = jnp.concatenate([grad_query, grad_kv.astype(bf16)], axis=1)

    qkv_part = lax.dot_general(
        grad_qkv, hidden, (((0,), (1,)), ((), ())), preferred_element_type=f32
    ).astype(bf16)
    out_part = lax.dot_general(
        attended, cotangent, (((0,), (0,)), ((), ())), preferred_element_type=f32
    ).astype(bf16)
    weight_rows = 4 * local_width
    weight_part = jnp.concatenate([qkv_part, out_part], axis=0).reshape(
        segments, weight_rows // segments, model_width
    )
    hidden_part = lax.dot_general(
        flat_weight, grad_qkv, (((1,), (1,)), ((), ())), preferred_element_type=f32
    )
    product = hidden_part * normed
    dots_part = jnp.sum(product * gain, axis=0, keepdims=True)
    gain_part = jnp.sum(product, axis=1).reshape(shares, 1, share_width)
    shared_hidden = hidden_part.astype(bf16).reshape(shares, share_width, tok_rows)
    dots_in, gain_in, weights_in, hidden_in = exchange(
        4,
        (dots_part, "mp", "direct"),
        (gain_part, "mp", "scatter"),
        (weight_part, "seg", "scatter"),
        (shared_hidden, "mp", "scatter"),
    )
    factor = (tok_rows * segments) ** (-0.5)
    weight_sum = (jnp.sum(weights_in.astype(f32), axis=0) * factor).astype(bf16)
    gain_sum = jnp.sum(gain_in, axis=0) * factor
    gains_all, weights_all = exchange(5, (gain_sum, "seg", "direct"), (weight_sum, "seg", "gather"))
    weights_all = weights_all.reshape(weight_rows, model_width).astype(f32)
    qkv_grad = weights_all[: 3 * local_width].T.reshape(model_width, 3, local_width)
    out_grad = weights_all[3 * local_width :]
    gain_grad = jnp.sum(gains_all, axis=0).reshape(share_width)

    grad_hidden = jnp.sum(hidden_in.astype(f32), axis=0)
    mean = jnp.sum(dots_in, axis=0) / model_width
    scaled = grad_hidden * columns_here(gain, 0)
    token_grads = columns_here(cotangent, 1).astype(f32) + (
        inv_rms * (scaled - columns_here(normed, 0) * mean)
    ).T
    return (token_grads, qkv_grad, out_grad, gain_grad)


def solution(mesh):
    placed = (
        P("seg", None),
        P("seg"),
        P("seg"),
        P("seg"),
        P("seg", None),
        P(),
        P(),
        P(None, None, "mp"),
        P("mp", None),
        P("seg", None),
    )
    return jax.shard_map(
        per_device,
        mesh=mesh,
        in_specs=placed,
        out_specs=(P("seg", "mp"), P(None, None, "mp"), P("mp", None), P("mp")),
        check_vma=False,
    )
```

```python
import jax
import jax.numpy as jnp
from jax import lax
from jax.experimental import pallas as pl
from jax.experimental.pallas import tpu as pltpu
from jax.sharding import PartitionSpec as P

DH = 64
R = 128
EPSILON = 1e-06
MESH = pl.DeviceIdType.MESH


def chunks_of(array):
    return next(n for n in (3, 2, 1) if array.shape[0] % (16 * n) == 0 or n == 1)


def exchange(collective_id, *parts):
    arrays = [part[0] for part in parts]
    axes = sorted({part[1] for part in parts})
    counts = {axis: lax.axis_size(axis) for axis in axes}
    shapes, slots, pairs = [], [], []
    for array, axis, kind in parts:
        count = counts[axis]
        lead = (count,) if kind in ("gather", "direct") else ()
        shape = lead + array.shape
        if kind == "reduce":
            shape = (count // 2,) + array.shape[1:]
            pairs.append(pltpu.VMEM(shape, array.dtype))
            pairs.append(pltpu.VMEM(shape, array.dtype))
        shapes.append(jax.ShapeDtypeStruct(shape, array.dtype))
        slots.append(
            {
                "scatter": count,
                "direct": count,
                "reduce": count,
                "gather": 2 * count * chunks_of(array),
            }.get(kind, 1)
        )
    number = len(parts)

    def remote(source, target, sends, receives, slot, axis, peer):
        return pltpu.make_async_remote_copy(
            src_ref=source,
            dst_ref=target,
            send_sem=sends.at[slot],
            recv_sem=receives.at[slot],
            device_id={axis: peer},
            device_id_type=MESH,
        )

    def scatter(source, target, sends, receives, axis, split):
        here, count = lax.axis_index(axis), counts[axis]
        copies = []
        for step in range(1, count):
            peer = lax.rem(here + step, count)
            block = source.at[peer] if split else source
            copies.append(remote(block, target.at[here], sends, receives, step, axis, peer))
        block = source.at[here] if split else source
        copies.append(pltpu.make_async_copy(block, target.at[here], sends.at[0]))
        for copy in copies:
            copy.start()

        def finish():
            for copy in copies:
                copy.wait()

        return (lambda step: None), finish

    def reduce(source, target, sends, receives, axis, came, summed):
        here, count = lax.axis_index(axis), counts[axis]
        line = count // 2
        outer, inner = here // 2, lax.rem(here, 2)
        order = [*range(1, line), 0]

        def place(step):
            return lax.rem(outer + step, line)

        def to_partner(step):
            there = place(step)
            return remote(
                source.at[2 * there + 1 - inner],
                came.at[there],
                sends,
                receives,
                step,
                axis,
                2 * outer + 1 - inner,
            )

        def to_owner(step):
            there = place(step)
            return remote(
                summed.at[there],
                target.at[outer],
                sends,
                receives,
                line + step,
                axis,
                2 * there + inner,
            )

        for step in order:
            to_partner(step).start()

        def relay(turn):
            if turn > line:
                return
            step = order[turn - 1]
            there = place(step)
            to_partner(step).wait_recv()
            pair = source[2 * there + inner].astype(jnp.float32) + came[there].astype(jnp.float32)
            if step:
                summed[there] = pair.astype(summed.dtype)
                to_owner(step).start()
            else:
                target[outer] = pair.astype(target.dtype)

        def finish():
            for step in order:
                to_partner(step).wait_send()
                if step:
                    to_owner(step).wait()

        return relay, finish

    def shift(source, target, sends, receives, axis, forward):
        here, count = lax.axis_index(axis), counts[axis]
        step = 1 if forward else -1
        peer = lax.rem(here + step + count, count)
        has_peer = here < count - 1 if forward else here > 0
        has_source = here > 0 if forward else here < count - 1
        copy = remote(source, target, sends, receives, 0, axis, peer)
        pl.when(has_peer)(copy.start)

        def finish():
            pl.when(has_peer)(copy.wait_send)
            pl.when(has_source)(copy.wait_recv)

        return (lambda step: None), finish

    def gather(source, target, sends, receives, axis, chunk, height):
        base = 2 * counts[axis] * chunk
        piece = pl.ds(chunk * height, height)
        source, whole = source.at[piece], target
        here, count = lax.axis_index(axis), counts[axis]
        line = count // 2
        outer = here // 2
        partner = here + 1 - 2 * lax.rem(here, 2)
        ahead = lax.rem(here + 2, count)
        behind = lax.rem(here + count - 2, count)
        own = pltpu.make_async_copy(source, whole.at[here, piece], sends.at[base + line])

        def block(shift):
            return whole.at[lax.rem(here + 2 * shift + count, count), piece]

        def hand_on(shift, direction, step):
            peer = ahead if direction > 0 else behind
            slot = step if direction > 0 else line + step
            taken = source if shift == 0 else block(shift)
            return remote(taken, block(shift), sends, receives, base + slot, axis, peer)

        def hand_over(shift):
            slot = 2 * line + (shift if shift >= 0 else line - 1 - shift)
            taken = source if shift == 0 else block(shift)
            return remote(taken, block(shift), sends, receives, base + slot, axis, partner)

        def there(shift):
            place = outer + shift
            return (place >= 0) if shift < 0 else (place < line)

        if line > 1:
            pl.when(there(1))(hand_on(0, 1, 1).start)
            pl.when(there(-1))(hand_on(0, -1, 1).start)
        hand_over(0).start()
        own.start()

        def relay(step):
            if step < line:
                for direction in (1, -1):
                    came = -direction * step

                    @pl.when(there(came))
                    def _():
                        hand_on(came, direction, step).wait_recv()
                        if step < line - 1:
                            pl.when(there(direction))(hand_on(came, direction, step + 1).start)
                        hand_over(came).start()

        def finish():
            for step in range(1, line):
                for direction in (1, -1):
                    came = -direction * (step - 1)

                    @pl.when(there(direction) if step == 1 else there(came) & there(direction))
                    def _():
                        hand_on(came, direction, step).wait_send()

                    pl.when(there(direction * step))(hand_over(direction * step).wait)
            hand_over(0).wait()
            own.wait()

        return relay, finish

    def body(*refs):
        groups = [refs[i * number : (i + 1) * number] for i in range(4)]
        barrier = pltpu.get_barrier_semaphore()
        expected = 0
        for axis in axes:
            here, count = lax.axis_index(axis), counts[axis]
            for step in range(1, count):
                pl.semaphore_signal(
                    barrier,
                    inc=1,
                    device_id={axis: lax.rem(here + step, count)},
                    device_id_type=MESH,
                )
                expected += 1
        pl.semaphore_wait(barrier, expected)
        pending = []
        scratch = list(refs[4 * number :])
        for (array, axis, kind), *held in zip(parts, *groups):
            if kind in ("scatter", "direct"):
                pending.append(scatter(*held, axis, kind == "scatter"))
            elif kind == "gather":
                chunks = chunks_of(array)
                for chunk in range(chunks):
                    pending.append(gather(*held, axis, chunk, array.shape[0] // chunks))
            elif kind == "reduce":
                pending.append(reduce(*held, axis, scratch.pop(0), scratch.pop(0)))
            else:
                pending.append(shift(*held, axis, kind == "next"))
        for step in range(1, max(counts.values()) // 2 + 1):
            for relay, _ in pending:
                relay(step)
        for _, finish in pending:
            finish()

    return pl.pallas_call(
        body,
        out_shape=shapes,
        in_specs=[pl.BlockSpec(memory_space=pltpu.VMEM)] * number,
        out_specs=[pl.BlockSpec(memory_space=pltpu.VMEM)] * number,
        scratch_shapes=[pltpu.SemaphoreType.DMA((n,)) for n in slots] * 2 + pairs,
        compiler_params=pltpu.CompilerParams(collective_id=collective_id, has_side_effects=True),
        name=f"exchange_{collective_id}",
    )(*arrays)


def attention(queries, extended, grad_out, neighbours):
    tok_rows, width = queries.shape
    heads = width // DH
    rows = R
    span = rows + 2 * R
    scale = DH ** (-0.5)

    def body(q_ref, kv_ref, g_ref, near_ref, out_ref, dq_ref, grad_ref):
        step = pl.program_id(0)

        @pl.when(step == 0)
        def _():
            grad_ref[...] = jnp.zeros_like(grad_ref)

        start = pl.multiple_of(step * rows, rows)
        first = lax.axis_index("seg") * tok_rows - R + step * rows
        near = near_ref[...] - first
        places = lax.broadcasted_iota(jnp.int32, (rows, span), 1)
        allowed = near[:, 0:1] == places
        for column in range(1, near.shape[1]):
            allowed = allowed | (near[:, column : column + 1] == places)
        window = kv_ref[pl.ds(start, span), :]
        outs, dqs, dks, dvs = [], [], [], []
        for head in range(heads):
            part = slice(head * DH, (head + 1) * DH)
            q, g = q_ref[:, part], g_ref[:, part]
            k = window[:, part]
            v = window[:, width + head * DH : width + (head + 1) * DH]
            across = (((1,), (1,)), ((), ()))
            down = (((0,), (0,)), ((), ()))
            s = lax.dot_general(q, k, across, preferred_element_type=jnp.float32) * scale
            s = jnp.where(allowed, s, -jnp.inf)
            e = jnp.exp(s - jnp.max(s, axis=1, keepdims=True))
            p = e * (1.0 / jnp.sum(e, axis=1, keepdims=True))
            w = p.astype(jnp.bfloat16)
            o = jnp.dot(w, v, preferred_element_type=jnp.float32).astype(jnp.bfloat16)
            delta = jnp.sum(
                g.astype(jnp.float32) * o.astype(jnp.float32), axis=1, keepdims=True
            )
            gp = lax.dot_general(g, v, across, preferred_element_type=jnp.float32)
            ds = (p * (gp - delta) * scale).astype(jnp.bfloat16)
            outs.append(o)
            dqs.append(jnp.dot(ds, k, preferred_element_type=jnp.float32).astype(jnp.bfloat16))
            dks.append(lax.dot_general(ds, q, down, preferred_element_type=jnp.float32))
            dvs.append(lax.dot_general(w, g, down, preferred_element_type=jnp.float32))
        out_ref[...] = jnp.concatenate(outs, axis=1)
        dq_ref[...] = jnp.concatenate(dqs, axis=1)
        grad_ref[pl.ds(start, span), :] += jnp.concatenate(dks + dvs, axis=1)

    by_row = pl.BlockSpec((rows, width), lambda i: (i, 0))
    whole = pl.BlockSpec(extended.shape, lambda i: (0, 0))
    return pl.pallas_call(
        body,
        grid=(tok_rows // rows,),
        in_specs=[
            by_row,
            whole,
            by_row,
            pl.BlockSpec((rows, neighbours.shape[1]), lambda i: (i, 0)),
        ],
        out_specs=[by_row, by_row, whole],
        out_shape=[
            jax.ShapeDtypeStruct((tok_rows, width), jnp.bfloat16),
            jax.ShapeDtypeStruct((tok_rows, width), jnp.bfloat16),
            jax.ShapeDtypeStruct(extended.shape, jnp.float32),
        ],
        name="window_attention",
    )(queries, extended, grad_out, neighbours)


def per_device(
    patches,
    curve_owner,
    arrival_slot,
    patch_level,
    neighbours,
    level_embed,
    norm_gain,
    qkv_weight,
    out_weight,
    cotangent,
):
    segments = lax.axis_size("seg")
    shares = lax.axis_size("mp")
    tok_rows, model_width = patches.shape
    local_width = qkv_weight.shape[2]
    capacity = 2 * tok_rows // segments
    share_width = model_width // shares
    first_column = lax.axis_index("mp") * share_width
    bf16, f32 = jnp.bfloat16, jnp.float32

    def columns_here(array, dim):
        return lax.dynamic_slice_in_dim(array, first_column, share_width, dim)

    row = jnp.arange(tok_rows, dtype=jnp.int32)
    owner_hot = curve_owner[:, None] == jnp.arange(segments, dtype=jnp.int32)[None, :]
    before = (row[None, :] < row[:, None]).astype(bf16)
    counted = jnp.dot(before, owner_hot.astype(bf16), preferred_element_type=f32)
    row_ranks = jnp.sum(jnp.where(owner_hot, counted, 0.0), axis=1).astype(jnp.int32)
    slot_index = curve_owner * capacity + row_ranks
    slots = jnp.arange(segments * capacity, dtype=jnp.int32)
    sent_hot = (slot_index[:, None] == slots[None, :]).astype(bf16)
    packed = lax.dot_general(
        columns_here(patches, 1), sent_hot, (((0,), (0,)), ((), ())), preferred_element_type=f32
    ).astype(bf16)
    packed = packed.reshape(share_width, segments, capacity).transpose(1, 0, 2)
    (arrived,) = exchange(0, (packed, "seg", "scatter"))
    arrived = arrived.transpose(1, 0, 2).reshape(share_width, segments * capacity)
    taken_hot = (slots[:, None] == arrival_slot[None, :]).astype(bf16)
    routed = jnp.dot(arrived, taken_hot, preferred_element_type=f32).astype(bf16)
    (routed,) = exchange(1, (routed, "mp", "gather"))
    routed = routed.reshape(model_width, tok_rows)

    levels = jnp.arange(level_embed.shape[0], dtype=jnp.int32)
    level_hot = (levels[:, None] == patch_level[None, :]).astype(bf16)
    embedded = routed.astype(f32) + lax.dot_general(
        level_embed, level_hot, (((0,), (0,)), ((), ())), preferred_element_type=f32
    )
    inv_rms = lax.rsqrt(jnp.mean(embedded * embedded, axis=0, keepdims=True) + EPSILON)
    normed = embedded * inv_rms
    gain = norm_gain[:, None]
    hidden = (normed * gain).astype(bf16)
    flat_weight = qkv_weight.reshape(model_width, 3 * local_width)
    project = lax.dot_general(
        hidden, flat_weight, (((0,), (0,)), ((), ())), preferred_element_type=f32
    ).astype(bf16)
    queries = project[:, :local_width]
    key_value = project[:, local_width:]
    from_left, from_right = exchange(
        2, (key_value[tok_rows - R :], "seg", "next"), (key_value[:R], "seg", "prev")
    )
    segment = lax.axis_index("seg")
    from_left = jnp.where(segment > 0, from_left, 0)
    from_right = jnp.where(segment < segments - 1, from_right, 0)
    extended = jnp.concatenate([from_left, key_value, from_right], axis=0)
    grad_out = lax.dot_general(
        cotangent, out_weight, (((1,), (1,)), ((), ())), preferred_element_type=f32
    ).astype(bf16)
    attended, grad_query, grad_ext = attention(queries, extended, grad_out, neighbours)
    rim_left, rim_right = exchange(
        3,
        (grad_ext[tok_rows + R :].astype(bf16), "seg", "next"),
        (grad_ext[:R].astype(bf16), "seg", "prev"),
    )
    rim_left = jnp.where(segment > 0, rim_left, 0)
    rim_right = jnp.where(segment < segments - 1, rim_right, 0)
    grad_kv = jnp.concatenate(
        [
            grad_ext[R : 2 * R] + rim_left.astype(f32),
            grad_ext[2 * R : tok_rows],
            grad_ext[tok_rows : tok_rows + R] + rim_right.astype(f32),
        ],
        axis=0,
    )
    grad_qkv = jnp.concatenate([grad_query, grad_kv.astype(bf16)], axis=1)

    qkv_part = lax.dot_general(
        grad_qkv, hidden, (((0,), (1,)), ((), ())), preferred_element_type=f32
    ).astype(bf16)
    out_part = lax.dot_general(
        attended, cotangent, (((0,), (0,)), ((), ())), preferred_element_type=f32
    ).astype(bf16)
    weight_rows = 4 * local_width
    weight_part = jnp.concatenate([qkv_part, out_part], axis=0).reshape(
        segments, weight_rows // segments, model_width
    )
    hidden_part = lax.dot_general(
        flat_weight, grad_qkv, (((1,), (1,)), ((), ())), preferred_element_type=f32
    )
    product = hidden_part * normed
    dots_part = jnp.sum(product * gain, axis=0, keepdims=True)
    gain_part = jnp.sum(product, axis=1).reshape(shares, 1, share_width)
    shared_hidden = hidden_part.astype(bf16).reshape(shares, share_width, tok_rows)
    dots_in, gain_in, weights_in, hidden_in = exchange(
        4,
        (dots_part, "mp", "direct"),
        (gain_part, "mp", "scatter"),
        (weight_part, "seg", "reduce"),
        (shared_hidden, "mp", "scatter"),
    )
    factor = (tok_rows * segments) ** (-0.5)
    weight_sum = (jnp.sum(weights_in.astype(f32), axis=0) * factor).astype(bf16)
    gain_sum = jnp.sum(gain_in, axis=0) * factor
    gains_all, weights_all = exchange(5, (gain_sum, "seg", "direct"), (weight_sum, "seg", "gather"))
    weights_all = weights_all.reshape(weight_rows, model_width).astype(f32)
    qkv_grad = weights_all[: 3 * local_width].T.reshape(model_width, 3, local_width)
    out_grad = weights_all[3 * local_width :]
    gain_grad = jnp.sum(gains_all, axis=0).reshape(share_width)

    grad_hidden = jnp.sum(hidden_in.astype(f32), axis=0)
    mean = jnp.sum(dots_in, axis=0) / model_width
    scaled = grad_hidden * columns_here(gain, 0)
    token_grads = columns_here(cotangent, 1).astype(f32) + (
        inv_rms * (scaled - columns_here(normed, 0) * mean)
    ).T
    return (token_grads, qkv_grad, out_grad, gain_grad)


def solution(mesh):
    placed = (
        P("seg", None),
        P("seg"),
        P("seg"),
        P("seg"),
        P("seg", None),
        P(),
        P(),
        P(None, None, "mp"),
        P("mp", None),
        P("seg", None),
    )
    return jax.shard_map(
        per_device,
        mesh=mesh,
        in_specs=placed,
        out_specs=(P("seg", "mp"), P(None, None, "mp"), P("mp", None), P("mp")),
        check_vma=False,
    )
```

```python
import jax
import jax.numpy as jnp
from jax import lax
from jax.experimental import pallas as pl
from jax.experimental.pallas import tpu as pltpu
from jax.sharding import PartitionSpec as P

DH = 64
R = 128
EPSILON = 1e-06
MESH = pl.DeviceIdType.MESH


def chunks_of(array):
    return next(n for n in (3, 2, 1) if array.shape[0] % (16 * n) == 0 or n == 1)


def exchange(collective_id, *parts):
    arrays = [part[0] for part in parts]
    axes = sorted({part[1] for part in parts})
    counts = {axis: lax.axis_size(axis) for axis in axes}
    shapes, slots, pairs = [], [], []
    for array, axis, kind in parts:
        count = counts[axis]
        lead = (count,) if kind in ("gather", "direct") else ()
        shape = lead + array.shape
        if kind == "reduce":
            shape = (count // 2,) + array.shape[1:]
            pairs.append(pltpu.VMEM(shape, array.dtype))
            pairs.append(pltpu.VMEM(shape, array.dtype))
        shapes.append(jax.ShapeDtypeStruct(shape, array.dtype))
        slots.append(
            {
                "scatter": count,
                "direct": count,
                "reduce": count,
                "gather": 2 * count * chunks_of(array),
            }.get(kind, 1)
        )
    number = len(parts)

    def remote(source, target, sends, receives, slot, axis, peer):
        return pltpu.make_async_remote_copy(
            src_ref=source,
            dst_ref=target,
            send_sem=sends.at[slot],
            recv_sem=receives.at[slot],
            device_id={axis: peer},
            device_id_type=MESH,
        )

    def scatter(source, target, sends, receives, axis, split):
        here, count = lax.axis_index(axis), counts[axis]
        copies = []
        for step in range(1, count):
            peer = lax.rem(here + step, count)
            block = source.at[peer] if split else source
            copies.append(remote(block, target.at[here], sends, receives, step, axis, peer))
        block = source.at[here] if split else source
        copies.append(pltpu.make_async_copy(block, target.at[here], sends.at[0]))
        for copy in copies:
            copy.start()

        def finish():
            for copy in copies:
                copy.wait()

        return (lambda step: None), finish

    def reduce(source, target, sends, receives, axis, came, summed):
        here, count = lax.axis_index(axis), counts[axis]
        line = count // 2
        outer, inner = here // 2, lax.rem(here, 2)
        order = [*range(1, line), 0]

        def place(step):
            return lax.rem(outer + step, line)

        def to_partner(step):
            there = place(step)
            return remote(
                source.at[2 * there + 1 - inner],
                came.at[there],
                sends,
                receives,
                step,
                axis,
                2 * outer + 1 - inner,
            )

        def to_owner(step):
            there = place(step)
            return remote(
                summed.at[there],
                target.at[outer],
                sends,
                receives,
                line + step,
                axis,
                2 * there + inner,
            )

        for step in order:
            to_partner(step).start()

        def relay(turn):
            if turn > line:
                return
            step = order[turn - 1]
            there = place(step)
            to_partner(step).wait_recv()
            pair = source[2 * there + inner].astype(jnp.float32) + came[there].astype(jnp.float32)
            if step:
                summed[there] = pair.astype(summed.dtype)
                to_owner(step).start()
            else:
                target[outer] = pair.astype(target.dtype)

        def finish():
            for step in order:
                to_partner(step).wait_send()
                if step:
                    to_owner(step).wait()

        return relay, finish

    def shift(source, target, sends, receives, axis, forward):
        here, count = lax.axis_index(axis), counts[axis]
        step = 1 if forward else -1
        peer = lax.rem(here + step + count, count)
        has_peer = here < count - 1 if forward else here > 0
        has_source = here > 0 if forward else here < count - 1
        copy = remote(source, target, sends, receives, 0, axis, peer)
        pl.when(has_peer)(copy.start)

        def finish():
            pl.when(has_peer)(copy.wait_send)
            pl.when(has_source)(copy.wait_recv)

        return (lambda step: None), finish

    def gather(source, target, sends, receives, axis, chunk, height):
        base = 2 * counts[axis] * chunk
        piece = pl.ds(chunk * height, height)
        source, whole = source.at[piece], target
        here, count = lax.axis_index(axis), counts[axis]
        line = count // 2
        outer = here // 2
        partner = here + 1 - 2 * lax.rem(here, 2)
        ahead = lax.rem(here + 2, count)
        behind = lax.rem(here + count - 2, count)
        own = pltpu.make_async_copy(source, whole.at[here, piece], sends.at[base + line])

        def block(shift):
            return whole.at[lax.rem(here + 2 * shift + count, count), piece]

        def hand_on(shift, direction, step):
            peer = ahead if direction > 0 else behind
            slot = step if direction > 0 else line + step
            taken = source if shift == 0 else block(shift)
            return remote(taken, block(shift), sends, receives, base + slot, axis, peer)

        def hand_over(shift):
            slot = 2 * line + (shift if shift >= 0 else line - 1 - shift)
            taken = source if shift == 0 else block(shift)
            return remote(taken, block(shift), sends, receives, base + slot, axis, partner)

        def there(shift):
            place = outer + shift
            return (place >= 0) if shift < 0 else (place < line)

        if line > 1:
            pl.when(there(1))(hand_on(0, 1, 1).start)
            pl.when(there(-1))(hand_on(0, -1, 1).start)
        hand_over(0).start()
        own.start()

        def relay(step):
            if step < line:
                for direction in (1, -1):
                    came = -direction * step

                    @pl.when(there(came))
                    def _():
                        hand_on(came, direction, step).wait_recv()
                        if step < line - 1:
                            pl.when(there(direction))(hand_on(came, direction, step + 1).start)
                        hand_over(came).start()

        def finish():
            for step in range(1, line):
                for direction in (1, -1):
                    came = -direction * (step - 1)

                    @pl.when(there(direction) if step == 1 else there(came) & there(direction))
                    def _():
                        hand_on(came, direction, step).wait_send()

                    pl.when(there(direction * step))(hand_over(direction * step).wait)
            hand_over(0).wait()
            own.wait()

        return relay, finish

    def body(*refs):
        groups = [refs[i * number : (i + 1) * number] for i in range(4)]
        barrier = pltpu.get_barrier_semaphore()
        expected = 0
        for axis in axes:
            here, count = lax.axis_index(axis), counts[axis]
            for step in range(1, count):
                pl.semaphore_signal(
                    barrier,
                    inc=1,
                    device_id={axis: lax.rem(here + step, count)},
                    device_id_type=MESH,
                )
                expected += 1
        pl.semaphore_wait(barrier, expected)
        pending = []
        scratch = list(refs[4 * number :])
        for (array, axis, kind), *held in zip(parts, *groups):
            if kind in ("scatter", "direct"):
                pending.append(scatter(*held, axis, kind == "scatter"))
            elif kind == "gather":
                chunks = chunks_of(array)
                for chunk in range(chunks):
                    pending.append(gather(*held, axis, chunk, array.shape[0] // chunks))
            elif kind == "reduce":
                pending.append(reduce(*held, axis, scratch.pop(0), scratch.pop(0)))
            else:
                pending.append(shift(*held, axis, kind == "next"))
        for step in range(1, max(counts.values()) // 2 + 1):
            for relay, _ in pending:
                relay(step)
        for _, finish in pending:
            finish()

    return pl.pallas_call(
        body,
        out_shape=shapes,
        in_specs=[pl.BlockSpec(memory_space=pltpu.VMEM)] * number,
        out_specs=[pl.BlockSpec(memory_space=pltpu.VMEM)] * number,
        scratch_shapes=[pltpu.SemaphoreType.DMA((n,)) for n in slots] * 2 + pairs,
        compiler_params=pltpu.CompilerParams(collective_id=collective_id, has_side_effects=True),
        name=f"exchange_{collective_id}",
    )(*arrays)


def attention(queries, extended, grad_out, neighbours):
    tok_rows, width = queries.shape
    heads = width // DH
    rows = R
    span = rows + 2 * R
    scale = DH ** (-0.5)

    def body(q_ref, kv_ref, g_ref, near_ref, out_ref, dq_ref, grad_ref):
        step = pl.program_id(0)

        @pl.when(step == 0)
        def _():
            grad_ref[...] = jnp.zeros_like(grad_ref)

        start = pl.multiple_of(step * rows, rows)
        first = lax.axis_index("seg") * tok_rows - R + step * rows
        near = near_ref[...] - first
        places = lax.broadcasted_iota(jnp.int32, (rows, span), 1)
        allowed = near[:, 0:1] == places
        for column in range(1, near.shape[1]):
            allowed = allowed | (near[:, column : column + 1] == places)
        window = kv_ref[pl.ds(start, span), :]
        outs, dqs, dks, dvs = [], [], [], []
        for head in range(heads):
            part = slice(head * DH, (head + 1) * DH)
            q, g = q_ref[:, part], g_ref[:, part]
            k = window[:, part]
            v = window[:, width + head * DH : width + (head + 1) * DH]
            across = (((1,), (1,)), ((), ()))
            down = (((0,), (0,)), ((), ()))
            s = lax.dot_general(q, k, across, preferred_element_type=jnp.float32) * scale
            s = jnp.where(allowed, s, -jnp.inf)
            e = jnp.exp(s - jnp.max(s, axis=1, keepdims=True))
            p = e * (1.0 / jnp.sum(e, axis=1, keepdims=True))
            w = p.astype(jnp.bfloat16)
            o = jnp.dot(w, v, preferred_element_type=jnp.float32).astype(jnp.bfloat16)
            delta = jnp.sum(
                g.astype(jnp.float32) * o.astype(jnp.float32), axis=1, keepdims=True
            )
            gp = lax.dot_general(g, v, across, preferred_element_type=jnp.float32)
            ds = (p * (gp - delta) * scale).astype(jnp.bfloat16)
            outs.append(o)
            dqs.append(jnp.dot(ds, k, preferred_element_type=jnp.float32).astype(jnp.bfloat16))
            dks.append(lax.dot_general(ds, q, down, preferred_element_type=jnp.float32))
            dvs.append(lax.dot_general(w, g, down, preferred_element_type=jnp.float32))
        out_ref[...] = jnp.concatenate(outs, axis=1)
        dq_ref[...] = jnp.concatenate(dqs, axis=1)
        grad_ref[pl.ds(start, span), :] += jnp.concatenate(dks + dvs, axis=1)

    by_row = pl.BlockSpec((rows, width), lambda i: (i, 0))
    whole = pl.BlockSpec(extended.shape, lambda i: (0, 0))
    return pl.pallas_call(
        body,
        grid=(tok_rows // rows,),
        in_specs=[
            by_row,
            whole,
            by_row,
            pl.BlockSpec((rows, neighbours.shape[1]), lambda i: (i, 0)),
        ],
        out_specs=[by_row, by_row, whole],
        out_shape=[
            jax.ShapeDtypeStruct((tok_rows, width), jnp.bfloat16),
            jax.ShapeDtypeStruct((tok_rows, width), jnp.bfloat16),
            jax.ShapeDtypeStruct(extended.shape, jnp.float32),
        ],
        name="window_attention",
    )(queries, extended, grad_out, neighbours)


def per_device(
    patches,
    curve_owner,
    arrival_slot,
    patch_level,
    neighbours,
    level_embed,
    norm_gain,
    qkv_weight,
    out_weight,
    cotangent,
):
    segments = lax.axis_size("seg")
    shares = lax.axis_size("mp")
    tok_rows, model_width = patches.shape
    local_width = qkv_weight.shape[2]
    capacity = 2 * tok_rows // segments
    share_width = model_width // shares
    first_column = lax.axis_index("mp") * share_width
    bf16, f32 = jnp.bfloat16, jnp.float32

    def columns_here(array, dim):
        return lax.dynamic_slice_in_dim(array, first_column, share_width, dim)

    row = jnp.arange(tok_rows, dtype=jnp.int32)
    owner_hot = curve_owner[:, None] == jnp.arange(segments, dtype=jnp.int32)[None, :]
    before = (row[None, :] < row[:, None]).astype(bf16)
    counted = jnp.dot(before, owner_hot.astype(bf16), preferred_element_type=f32)
    row_ranks = jnp.sum(jnp.where(owner_hot, counted, 0.0), axis=1).astype(jnp.int32)
    slot_index = curve_owner * capacity + row_ranks
    slots = jnp.arange(segments * capacity, dtype=jnp.int32)
    sent_hot = (slot_index[:, None] == slots[None, :]).astype(bf16)
    packed = lax.dot_general(
        columns_here(patches, 1), sent_hot, (((0,), (0,)), ((), ())), preferred_element_type=f32
    ).astype(bf16)
    packed = packed.reshape(share_width, segments, capacity).transpose(1, 0, 2)
    (arrived,) = exchange(0, (packed, "seg", "scatter"))
    arrived = arrived.transpose(1, 0, 2).reshape(share_width, segments * capacity)
    taken_hot = (slots[:, None] == arrival_slot[None, :]).astype(bf16)
    routed = jnp.dot(arrived, taken_hot, preferred_element_type=f32).astype(bf16)
    (routed,) = exchange(1, (routed, "mp", "gather"))
    routed = routed.reshape(model_width, tok_rows)

    levels = jnp.arange(level_embed.shape[0], dtype=jnp.int32)
    level_hot = (levels[:, None] == patch_level[None, :]).astype(bf16)
    embedded = routed.astype(f32) + lax.dot_general(
        level_embed, level_hot, (((0,), (0,)), ((), ())), preferred_element_type=f32
    )
    inv_rms = lax.rsqrt(jnp.mean(embedded * embedded, axis=0, keepdims=True) + EPSILON)
    normed = embedded * inv_rms
    gain = norm_gain[:, None]
    hidden = (normed * gain).astype(bf16)
    flat_weight = qkv_weight.reshape(model_width, 3 * local_width)
    project = lax.dot_general(
        hidden, flat_weight, (((0,), (0,)), ((), ())), preferred_element_type=f32
    ).astype(bf16)
    queries = project[:, :local_width]
    key_value = project[:, local_width:]
    from_left, from_right = exchange(
        2, (key_value[tok_rows - R :], "seg", "next"), (key_value[:R], "seg", "prev")
    )
    segment = lax.axis_index("seg")
    from_left = jnp.where(segment > 0, from_left, 0)
    from_right = jnp.where(segment < segments - 1, from_right, 0)
    extended = jnp.concatenate([from_left, key_value, from_right], axis=0)
    grad_out = lax.dot_general(
        cotangent, out_weight, (((1,), (1,)), ((), ())), preferred_element_type=f32
    ).astype(bf16)
    attended, grad_query, grad_ext = attention(queries, extended, grad_out, neighbours)
    rim_left, rim_right = exchange(
        3,
        (grad_ext[tok_rows + R :].astype(bf16), "seg", "next"),
        (grad_ext[:R].astype(bf16), "seg", "prev"),
    )
    rim_left = jnp.where(segment > 0, rim_left, 0)
    rim_right = jnp.where(segment < segments - 1, rim_right, 0)
    grad_kv = jnp.concatenate(
        [
            grad_ext[R : 2 * R] + rim_left.astype(f32),
            grad_ext[2 * R : tok_rows],
            grad_ext[tok_rows : tok_rows + R] + rim_right.astype(f32),
        ],
        axis=0,
    )
    grad_qkv = jnp.concatenate([grad_query, grad_kv.astype(bf16)], axis=1)

    qkv_part = lax.dot_general(
        grad_qkv, hidden, (((0,), (1,)), ((), ())), preferred_element_type=f32
    ).astype(bf16)
    out_part = lax.dot_general(
        attended, cotangent, (((0,), (0,)), ((), ())), preferred_element_type=f32
    ).astype(bf16)
    weight_rows = 4 * local_width
    weight_part = jnp.concatenate([qkv_part, out_part], axis=0).reshape(
        segments, weight_rows // segments, model_width
    )
    hidden_part = lax.dot_general(
        flat_weight, grad_qkv, (((1,), (1,)), ((), ())), preferred_element_type=f32
    )
    product = hidden_part * normed
    dots_part = jnp.sum(product * gain, axis=0, keepdims=True)
    gain_part = jnp.sum(product, axis=1).reshape(shares, 1, share_width)
    shared_hidden = hidden_part.astype(bf16).reshape(shares, share_width, tok_rows)
    dots_in, gain_in, weights_in, hidden_in = exchange(
        4,
        (dots_part, "mp", "direct"),
        (gain_part, "mp", "scatter"),
        (weight_part, "seg", "reduce"),
        (shared_hidden, "mp", "reduce"),
    )
    factor = (tok_rows * segments) ** (-0.5)
    weight_sum = (jnp.sum(weights_in.astype(f32), axis=0) * factor).astype(bf16)
    gain_sum = jnp.sum(gain_in, axis=0) * factor
    gains_all, weights_all = exchange(5, (gain_sum, "seg", "direct"), (weight_sum, "seg", "gather"))
    weights_all = weights_all.reshape(weight_rows, model_width).astype(f32)
    qkv_grad = weights_all[: 3 * local_width].T.reshape(model_width, 3, local_width)
    out_grad = weights_all[3 * local_width :]
    gain_grad = jnp.sum(gains_all, axis=0).reshape(share_width)

    grad_hidden = jnp.sum(hidden_in.astype(f32), axis=0)
    mean = jnp.sum(dots_in, axis=0) / model_width
    scaled = grad_hidden * columns_here(gain, 0)
    token_grads = columns_here(cotangent, 1).astype(f32) + (
        inv_rms * (scaled - columns_here(normed, 0) * mean)
    ).T
    return (token_grads, qkv_grad, out_grad, gain_grad)


def solution(mesh):
    placed = (
        P("seg", None),
        P("seg"),
        P("seg"),
        P("seg"),
        P("seg", None),
        P(),
        P(),
        P(None, None, "mp"),
        P("mp", None),
        P("seg", None),
    )
    return jax.shard_map(
        per_device,
        mesh=mesh,
        in_specs=placed,
        out_specs=(P("seg", "mp"), P(None, None, "mp"), P("mp", None), P("mp")),
        check_vma=False,
    )
```
